32 devices in a mesh: section: 2 (over x), patch: 4 (over z), fsdp: 4 (over y, core).
Axes of the slice: x: 2, y: 2, z: 4, core: 2. Of those that a mesh axis runs over, the one named last changes fastest.
Arguments:
- latent: float32 [8, 4, 256, 64], P('fsdp', 'patch', 'section'), may hold values from -60 to 60
- counts: int32 [8, 4], P('fsdp'), may hold values from 64 to 256, as said below
- steps_idx: int32 [8], P('fsdp'), may hold values from 0 to 49
- embed_weight: bfloat16 [64, 1536], replicated, may hold values from -0.75 to 0.75
- wqkv: bfloat16 [2, 1536, 4608], P('section', 'fsdp'), may hold values from -0.15625 to 0.15625
- wo: bfloat16 [2, 1536, 1536], P('section', 'fsdp'), may hold values from -0.15625 to 0.15625
- qk_gain: float32 [2, 3072], P('section'), may hold values from 0.1 to 1.9
- modulation: float32 [2, 50, 4608], P('section'), may hold values from -3 to 3
- head_mod: float32 [50, 3072], replicated, may hold values from -3 to 3
- head_weight: bfloat16 [1536, 64], replicated, may hold values from -0.15625 to 0.15625
- stale_cache: bfloat16 [2, 8, 4, 256, 3072], P('section', 'fsdp', 'patch'), may hold values from -210 to 210
Outputs:
- velocity: float32 [8, 4, 256, 64], P('fsdp', 'patch', 'section')
- new_latent: float32 [8, 4, 256, 64], P('fsdp', 'patch', 'section')
- cache_out: bfloat16 [2, 8, 4, 256, 3072], P('section', 'fsdp', 'patch')
The draws below stay inside these ranges and needn't reach their ends.
Inputs may be any that keep to these rules, and one draw needn't show every extreme that they name: `counts`: in every video one patch holds exactly 256 tokens.
All inputs are finite; a program needn't handle non-finite values.
Results may differ from the reference program's by a relative error of at most 0.0071.
Values may be sent and summed in bfloat16 or wider, within the bound.
A program may use at most 192 MiB of HBM per device.

```python
import math
import jax
import jax.numpy as jnp
from jax import lax

D = 1536
HEADS = 12
HD = 128
CH = 64
P_SIZE = 256
TSTEPS = 50
LAYERS = 2
VIDEOS = 8
N_PATCH = 4


def draw_latent(key, part):
    array_shape = (VIDEOS, N_PATCH, P_SIZE, CH)
    key_base = jax.random.fold_in(key, 0)
    normal_draw = jax.random.normal(key_base, array_shape, jnp.float32)
    return jnp.clip(normal_draw, -4.0, 4.0)


def draw_counts(key, part):
    key_count, key_full = jax.random.split(key)
    drawn_counts = jax.random.randint(key_count, (VIDEOS, N_PATCH), P_SIZE // 4, P_SIZE + 1)
    full_patch = jax.random.randint(key_full, (VIDEOS,), 0, N_PATCH)
    return jnp.where(jnp.arange(N_PATCH)[None, :] == full_patch[:, None], P_SIZE, drawn_counts).astype(jnp.int32)


def draw_stale_cache(key, part):
    array_shape = (LAYERS, VIDEOS, N_PATCH, P_SIZE, 2 * D)
    key_base = jax.random.fold_in(key, 0)
    base_draw = jnp.clip(jax.random.normal(key_base, array_shape, jnp.float32), -4.0, 4.0)
    return base_draw.astype(jnp.bfloat16)


def touch_ends(values, key, low, largest):
    longest = values.shape.index(max(values.shape))
    spots = []
    for shift in (0, 1):
        where = [jax.random.randint(jax.random.fold_in(key, axis), (), 0, length) for axis, length in enumerate(values.shape)]
        where[longest] = (where[longest] + shift) % values.shape[longest]
        spots.append(tuple(where))
    return values.at[spots[0]].set(low).at[spots[1]].set(largest)


def level_of(own_key, dims, pieces, least, high):
    def one(position, blocks):
        heights = jax.random.uniform(jax.random.fold_in(jax.random.fold_in(own_key, 6), position), (blocks,), jnp.float32, least / len(pieces), high / len(pieces))
        return jnp.repeat(jnp.exp(heights), dims[position] // blocks).reshape((-1,) + (1,) * (len(dims) - position - 1))

    loudness = one(*pieces[0])
    for cut in pieces[1:]:
        loudness = loudness * one(*cut)
    return loudness


def noise(stream_key, extent, width, reach, cuts=(), kind=jnp.bfloat16):
    level = level_of(stream_key, extent, cuts, -0.22, 0.18) if cuts else 1.0
    drawn = jax.random.normal(stream_key, extent, jnp.float32) * width * level
    return jnp.minimum(jnp.maximum(drawn, -reach), reach).astype(kind)


def setup_inputs(seed: int = 0) -> dict:
    key_list = jax.random.split(jax.random.key(seed), 12)
    return {
        "latent": draw_latent(jax.random.fold_in(key_list[11], 71), 0),
        "counts": draw_counts(jax.random.fold_in(key_list[11], 71), 0),
        "steps_idx": touch_ends(jax.random.randint(key_list[2], (VIDEOS,), 0, TSTEPS), jax.random.fold_in(key_list[2], 1), 0, TSTEPS - 1).astype(jnp.int32),
        "embed_weight": noise(key_list[3], (CH, D), CH ** -0.5, 0.75),
        "wqkv": noise(key_list[4], (LAYERS, D, 3 * D), D ** -0.5, 0.15625, ((0, 2), (1, 4))),
        "wo": noise(key_list[5], (LAYERS, D, D), D ** -0.5, 0.15625, ((0, 2), (1, 4))),
        "qk_gain": jnp.clip(1.0 + 0.18 * jax.random.normal(key_list[6], (LAYERS, 2 * D), jnp.float32), 0.1, 1.9),
        "modulation": noise(key_list[7], (LAYERS, TSTEPS, 3 * D), 0.5, 3.0, ((0, 2),), jnp.float32),
        "head_mod": noise(key_list[8], (TSTEPS, 2 * D), 0.5, 3.0, (), jnp.float32),
        "head_weight": noise(key_list[9], (D, CH), D ** -0.5, 0.15625),
        "stale_cache": draw_stale_cache(jax.random.fold_in(key_list[11], 71), 0),
    }


EPS = 1e-06

def layer_norm(hidden):
    center = hidden - lax.optimization_barrier(jnp.mean(hidden, axis=-1, keepdims=True))
    return center * lax.rsqrt(lax.optimization_barrier(jnp.mean(center * center, axis=-1, keepdims=True)) + EPS)

def rms_norm(values_in, gain_vec):
    return values_in * lax.rsqrt(lax.optimization_barrier(jnp.mean(values_in * values_in, axis=-1, keepdims=True)) + EPS) * gain_vec

def sigma_of(step_float):
    remain = 1.0 - step_float / TSTEPS
    return 5.0 * remain / (1.0 + 4.0 * remain)

def attend(queries, key_rows, value_rows, key_live):
    query_heads = queries.reshape(queries.shape[0], HEADS, HD).astype(jnp.float32)
    key_heads = key_rows.reshape(key_rows.shape[0], HEADS, HD).astype(jnp.float32)
    value_heads = value_rows.reshape(value_rows.shape[0], HEADS, HD).astype(jnp.float32)
    scores = jnp.einsum('qhd,khd->hqk', query_heads, key_heads) / math.sqrt(HD)
    scores = jnp.where(key_live[None, None, :], scores, -jnp.inf)
    top_score = lax.optimization_barrier(jnp.max(scores, axis=-1, keepdims=True))
    exp_scores = jnp.exp(scores - top_score)
    denom_sum = lax.optimization_barrier(jnp.sum(exp_scores, axis=-1))
    weights = lax.optimization_barrier(exp_scores.astype(jnp.bfloat16)).astype(jnp.float32)
    mixed_out = jnp.einsum('hqk,khd->qhd', weights, value_heads) / jnp.transpose(denom_sum)[:, :, None]
    return mixed_out.reshape(queries.shape[0], HEADS * HD).astype(jnp.bfloat16)

def reference(latent, counts, steps_idx, embed_weight, wqkv, wo, qk_gain, modulation, head_mod, head_weight, stale_cache):

    def video_step(inputs):
        latent_v, counts_v, step_v, stale_v = inputs
        live = jnp.arange(P_SIZE)[None, :] < counts_v[:, None]
        hidden = jnp.dot(latent_v.astype(jnp.bfloat16).reshape(-1, CH), embed_weight, preferred_element_type=jnp.float32)
        caches = []
        for layer_index in range(LAYERS):
            mod_row = modulation[layer_index, step_v]
            shift_vec, scale_vec, gate_vec = (mod_row[:D], mod_row[D:2 * D], mod_row[2 * D:])
            normed = (layer_norm(hidden) * (1.0 + scale_vec) + shift_vec).astype(jnp.bfloat16)
            projected = jnp.dot(normed, wqkv[layer_index], preferred_element_type=jnp.float32)
            queries = rms_norm(projected[:, :D], qk_gain[layer_index, :D]).astype(jnp.bfloat16)
            fresh_keys = rms_norm(projected[:, D:2 * D], qk_gain[layer_index, D:]).astype(jnp.bfloat16)
            fresh_values = projected[:, 2 * D:].astype(jnp.bfloat16)
            fresh_kv = jnp.concatenate([fresh_keys, fresh_values], axis=-1).reshape(N_PATCH, P_SIZE, 2 * D)
            caches.append(jnp.where(live[:, :, None], fresh_kv, jnp.zeros_like(fresh_kv)))
            query_blocks = queries.reshape(N_PATCH, P_SIZE, D)
            outputs = []
            for patch_slot in range(N_PATCH):
                seen_rows = stale_v[layer_index].at[patch_slot].set(fresh_kv[patch_slot]).reshape(N_PATCH * P_SIZE, 2 * D)
                outputs.append(attend(query_blocks[patch_slot], seen_rows[:, :D], seen_rows[:, D:], live.reshape(-1)))
            attended = jnp.concatenate(outputs, axis=0)
            hidden = hidden + gate_vec * jnp.dot(attended, wo[layer_index], preferred_element_type=jnp.float32)
            if layer_index + 1 < LAYERS:
                hidden = lax.optimization_barrier(hidden.astype(jnp.bfloat16)).astype(jnp.float32)
        head_row = head_mod[step_v]
        head_in = (layer_norm(hidden) * (1.0 + head_row[D:]) + head_row[:D]).astype(jnp.bfloat16)
        velocity = jnp.dot(head_in, head_weight, preferred_element_type=jnp.float32).reshape(N_PATCH, P_SIZE, CH)
        velocity = jnp.where(live[:, :, None], velocity, jnp.zeros_like(velocity))
        step_float = step_v.astype(jnp.float32)
        step_delta = sigma_of(step_float + 1.0) - sigma_of(step_float)
        return (velocity, latent_v + step_delta * velocity, jnp.stack(caches))
    velocity, new_latent, cache_all = lax.map(video_step, (latent, counts, steps_idx, jnp.moveaxis(stale_cache, 1, 0)))
    return (velocity, new_latent, jnp.moveaxis(cache_all, 0, 1))
```

```python
import math

import jax
import jax.numpy as jnp
from jax import lax
from jax.experimental import pallas as pl
from jax.experimental.pallas import tpu as pltpu
from jax.sharding import PartitionSpec as P

HEADS = 12
HD = 128
TSTEPS = 50


EPS = 1e-06


def shifted(shard, axis, by):
    devices = lax.axis_size(axis)
    pairs = [(i, i + by) for i in range(devices) if 0 <= i + by < devices]
    return lax.ppermute(shard, axis, pairs)


def layer_norm(hidden):
    center = hidden - jnp.mean(hidden, axis=-1, keepdims=True)
    return center * lax.rsqrt(jnp.mean(center * center, axis=-1, keepdims=True) + EPS)


def rms_norm(values_in, gain_vec):
    return (
        values_in
        * lax.rsqrt(jnp.mean(values_in * values_in, axis=-1, keepdims=True) + EPS)
        * gain_vec
    )


def sigma_of(step_float):
    remain = 1.0 - step_float / TSTEPS
    return 5.0 * remain / (1.0 + 4.0 * remain)


HEADS_STEP = 2


def attend_kernel(counts_ref, q_ref, *refs):
    blocks = (len(refs) - 1) // 2
    out_ref = refs[-1]
    for head in range(q_ref.shape[1] // HD):
        cols = slice(head * HD, (head + 1) * HD)
        query = q_ref[:, cols]
        scores = []
        for b in range(blocks):
            score = lax.dot_general(
                query, refs[2 * b][:, cols], (((1,), (1,)), ((), ())), preferred_element_type=jnp.float32
            ) * (1.0 / math.sqrt(HD))
            slot = lax.broadcasted_iota(jnp.int32, score.shape, 1)
            scores.append(jnp.where(slot < counts_ref[b], score, -jnp.inf))
        top = scores[0]
        for score in scores[1:]:
            top = jnp.maximum(top, score)
        top = jnp.max(top, axis=1, keepdims=True)
        total = None
        mixed = None
        for b in range(blocks):
            weight = jnp.exp(scores[b] - top)
            part = jnp.dot(
                weight.astype(jnp.bfloat16), refs[2 * b + 1][:, cols], preferred_element_type=jnp.float32
            )
            total = weight if total is None else total + weight
            mixed = part if mixed is None else mixed + part
        denom = jnp.sum(total, axis=1, keepdims=True)
        out_ref[:, cols] = (mixed / denom).astype(jnp.bfloat16)


def attend(queries, kv_blocks, block_counts):
    rows, model_width = queries.shape
    cols = HEADS_STEP * HD
    steps = model_width // cols
    specs = [pl.BlockSpec(memory_space=pltpu.SMEM), pl.BlockSpec((rows, cols), lambda h: (0, h))]
    operands = [block_counts, queries]
    for kv in kv_blocks:
        specs.append(pl.BlockSpec((kv.shape[0], cols), lambda h: (0, h)))
        specs.append(pl.BlockSpec((kv.shape[0], cols), lambda h: (0, h + steps)))
        operands += [kv, kv]
    keys = sum(kv.shape[0] for kv in kv_blocks)
    return pl.pallas_call(
        attend_kernel,
        grid=(steps,),
        in_specs=specs,
        out_specs=pl.BlockSpec((rows, cols), lambda h: (0, h)),
        out_shape=jax.ShapeDtypeStruct((rows, model_width), jnp.bfloat16),
        cost_estimate=pl.CostEstimate(
            flops=4 * rows * keys * model_width,
            bytes_accessed=4 * (rows + keys) * model_width,
            transcendentals=rows * keys * HEADS,
        ),
    )(*operands)


def body(
    latent,
    counts,
    steps_idx,
    embed_weight,
    wqkv,
    wo,
    qk_gain,
    modulation,
    head_mod,
    head_weight,
    stale_cache,
):
    section_index = lax.axis_index("section")
    own_patch = lax.axis_index("patch")
    first_section = section_index == 0
    videos = latent.shape[0]
    assert videos == 2 and lax.axis_size("section") == 2
    patch_rows = stale_cache.shape[3]
    model_width = embed_weight.shape[1]
    patch_count = counts.shape[1]
    early = section_index
    late = 1 - section_index
    rows_full = lax.all_gather(latent.astype(jnp.bfloat16), "section", axis=2, tiled=True)
    proj_full = lax.all_gather(wqkv[0], "fsdp", axis=0, tiled=True)
    out_full = lax.all_gather(wo[0], "fsdp", axis=0, tiled=True)
    ring = [(i, (i + 1) % patch_count) for i in range(patch_count)]

    def around(video, after=None):
        block = lax.dynamic_index_in_dim(stale_cache[0, :, 0], video, 0, keepdims=False)
        if after is not None:
            block, _ = lax.optimization_barrier((block, after))
        blocks = []
        for _ in range(patch_count - 1):
            block = lax.ppermute(block, "patch", ring)
            blocks.append(block)
        return blocks

    early_blocks = around(early)
    late_blocks = around(late, early_blocks[-1])

    start_hidden = jnp.dot(
        rows_full.reshape(-1, rows_full.shape[3]), embed_weight, preferred_element_type=jnp.float32
    )
    start_hidden = start_hidden.reshape(videos, patch_rows, model_width)
    step_onehot = (jnp.arange(TSTEPS, dtype=jnp.int32)[None, :] == steps_idx[:, None]).astype(
        jnp.float32
    )
    modulation_all = jnp.dot(step_onehot, modulation[0], precision=lax.Precision.HIGHEST)
    head_rows = jnp.dot(step_onehot, head_mod, precision=lax.Precision.HIGHEST)
    gain_rows = qk_gain[0]
    slot_iota = jnp.arange(patch_rows, dtype=jnp.int32)
    ring_counts = jnp.stack(
        [jnp.take(counts, (own_patch - k) % patch_count, axis=1) for k in range(patch_count)], axis=1
    )
    own_live = slot_iota[None, :] < ring_counts[:, :1]

    def layer(hidden, video, stale_blocks):
        mod = lax.dynamic_index_in_dim(modulation_all, video, 0)
        block_counts = lax.dynamic_index_in_dim(ring_counts, video, 0, keepdims=False)
        shift_vec = mod[:, :model_width]
        scale_vec = mod[:, model_width : 2 * model_width]
        gate_vec = mod[:, 2 * model_width :]
        normed = (layer_norm(hidden) * (1.0 + scale_vec) + shift_vec).astype(jnp.bfloat16)
        projected = jnp.dot(normed, proj_full, preferred_element_type=jnp.float32)
        queries = rms_norm(projected[:, :model_width], gain_rows[:model_width]).astype(jnp.bfloat16)
        keys = rms_norm(projected[:, model_width : 2 * model_width], gain_rows[model_width:])
        fresh_kv = jnp.concatenate(
            [keys.astype(jnp.bfloat16), projected[:, 2 * model_width :].astype(jnp.bfloat16)], axis=-1
        )
        attended = attend(queries, [fresh_kv] + stale_blocks, block_counts)
        update = jnp.dot(attended, out_full, preferred_element_type=jnp.float32)
        return hidden + gate_vec * update, fresh_kv

    def head(hidden, video):
        head_in = (
            layer_norm(hidden) * (1.0 + head_rows[video, None, model_width:])
            + head_rows[video, None, :model_width]
        ).astype(jnp.bfloat16)
        velocity = jnp.dot(head_in, head_weight, preferred_element_type=jnp.float32)
        velocity = jnp.where(own_live[video][:, None], velocity, jnp.zeros_like(velocity))
        half_rows = patch_rows // 2
        returned = shifted(velocity[:half_rows].astype(jnp.bfloat16), "section", -1)
        return jnp.where(first_section, returned.astype(jnp.float32), velocity[half_rows:])

    def forward(hidden):
        return shifted(hidden.astype(jnp.bfloat16), "section", 1).astype(jnp.float32)

    hidden_a, fresh_a = layer(start_hidden[0], early, early_blocks)
    received = forward(hidden_a)
    hidden_b, fresh_b = layer(jnp.where(first_section, start_hidden[1], received), late, late_blocks)
    received = forward(hidden_b)
    first_half = head(hidden_b, 0)
    hidden_c, fresh_c = layer(received, early, early_blocks)
    second_half = head(hidden_c, 1)
    cache_buf = jnp.stack(
        [jnp.where(first_section, fresh_a, fresh_b), jnp.where(first_section, fresh_b, fresh_c)]
    )
    cache_buf = jnp.where(own_live[..., None], cache_buf, jnp.zeros_like(cache_buf))
    mine_half = jnp.stack([first_half, second_half])
    step_float = steps_idx.astype(jnp.float32)
    step_delta = sigma_of(step_float + 1.0) - sigma_of(step_float)
    new_latent = latent + step_delta[:, None, None, None] * mine_half[:, None]
    return (mine_half[:, None], new_latent, cache_buf[None, :, None])


def solution(mesh):
    in_specs = (
        P("fsdp", "patch", "section", None),
        P("fsdp", None),
        P("fsdp"),
        P(),
        P("section", "fsdp", None),
        P("section", "fsdp", None),
        P("section", None),
        P("section", None, None),
        P(),
        P(),
        P("section", "fsdp", "patch", None, None),
    )
    out_specs = (
        P("fsdp", "patch", "section", None),
        P("fsdp", "patch", "section", None),
        P("section", "fsdp", "patch", None, None),
    )
    return jax.shard_map(body, mesh=mesh, in_specs=in_specs, out_specs=out_specs, check_vma=False)
```

```python
import math

import jax
import jax.numpy as jnp
from jax import lax
from jax.experimental import pallas as pl
from jax.experimental.pallas import tpu as pltpu
from jax.sharding import PartitionSpec as P

HEADS = 12
HD = 128
TSTEPS = 50


EPS = 1e-06


def shifted(shard, axis, by):
    devices = lax.axis_size(axis)
    pairs = [(i, i + by) for i in range(devices) if 0 <= i + by < devices]
    return lax.ppermute(shard, axis, pairs)


def layer_norm(hidden):
    center = hidden - jnp.mean(hidden, axis=-1, keepdims=True)
    return center * lax.rsqrt(jnp.mean(center * center, axis=-1, keepdims=True) + EPS)


def rms_norm(values_in, gain_vec):
    return (
        values_in
        * lax.rsqrt(jnp.mean(values_in * values_in, axis=-1, keepdims=True) + EPS)
        * gain_vec
    )


def sigma_of(step_float):
    remain = 1.0 - step_float / TSTEPS
    return 5.0 * remain / (1.0 + 4.0 * remain)


HEADS_STEP = 2
WIDE = 8


def attend_kernel(counts_ref, q_ref, *refs):
    blocks = (len(refs) - 1) // 2
    out_ref = refs[-1]
    slot = lax.broadcasted_iota(jnp.int32, (1, refs[0].shape[0]), 1)
    bias = [jnp.where(slot < counts_ref[b], 0.0, -jnp.inf) for b in range(blocks)]
    for head in range(q_ref.shape[1] // HD):
        cols = slice(head * HD, (head + 1) * HD)
        query = q_ref[:, cols]
        scores = []
        for b in range(blocks):
            score = lax.dot_general(
                query, refs[2 * b][:, cols], (((1,), (1,)), ((), ())), preferred_element_type=jnp.float32
            )
            scores.append(score * (math.log2(math.e) / math.sqrt(HD)) + bias[b])
        top = scores[0]
        for score in scores[1:]:
            top = jnp.maximum(top, score)
        top = jnp.max(top, axis=1, keepdims=True)
        total = None
        mixed = None
        for b in range(blocks):
            weight = jnp.exp2(scores[b] - top)
            part = jnp.dot(
                weight.astype(jnp.bfloat16), refs[2 * b + 1][:, cols], preferred_element_type=jnp.float32
            )
            total = weight if total is None else total + weight
            mixed = part if mixed is None else mixed + part
        denom = jnp.sum(total, axis=1, keepdims=True)
        out_ref[:, cols] = (mixed / denom).astype(jnp.bfloat16)


def attend(heads, queries, q_head, kv_blocks, block_counts):
    rows = queries.shape[0]
    cols = HEADS_STEP * HD
    steps = heads // HEADS_STEP

    def spec(array, first_head):
        first = first_head // HEADS_STEP
        return pl.BlockSpec((array.shape[0], cols), lambda h: (0, h + first))

    specs = [pl.BlockSpec(memory_space=pltpu.SMEM), spec(queries, q_head)]
    operands = [block_counts, queries]
    for kv, key_head, value_head in kv_blocks:
        specs += [spec(kv, key_head), spec(kv, value_head)]
        operands += [kv, kv]
    keys = sum(kv.shape[0] for kv, _, _ in kv_blocks)
    width = heads * HD
    return pl.pallas_call(
        attend_kernel,
        grid=(steps,),
        in_specs=specs,
        out_specs=pl.BlockSpec((rows, cols), lambda h: (0, h)),
        out_shape=jax.ShapeDtypeStruct((rows, width), jnp.bfloat16),
        cost_estimate=pl.CostEstimate(
            flops=4 * rows * keys * width,
            bytes_accessed=4 * (rows + keys) * width,
            transcendentals=rows * keys * heads,
        ),
    )(*operands)


def body(
    latent,
    counts,
    steps_idx,
    embed_weight,
    wqkv,
    wo,
    qk_gain,
    modulation,
    head_mod,
    head_weight,
    stale_cache,
):
    section_index = lax.axis_index("section")
    own_patch = lax.axis_index("patch")
    first_section = section_index == 0
    videos = latent.shape[0]
    assert videos == 2 and lax.axis_size("section") == 2 and counts.shape[1] == 4
    patch_rows = stale_cache.shape[3]
    model_width = embed_weight.shape[1]
    patch_count = counts.shape[1]
    early = section_index
    late = 1 - section_index
    rows_full = lax.all_gather(latent.astype(jnp.bfloat16), "section", axis=2, tiled=True)
    proj_full = lax.all_gather(wqkv[0], "fsdp", axis=0, tiled=True)
    out_full = lax.all_gather(wo[0], "fsdp", axis=0, tiled=True)
    ring = [(i, (i + 1) % patch_count) for i in range(patch_count)]
    early_blocks = []
    block = lax.dynamic_index_in_dim(stale_cache[0, :, 0], early, 0, keepdims=False)
    for _ in range(patch_count - 1):
        block = lax.ppermute(block, "patch", ring)
        early_blocks.append(block)

    start_hidden = jnp.dot(
        rows_full.reshape(-1, rows_full.shape[3]), embed_weight, preferred_element_type=jnp.float32
    )
    start_hidden = start_hidden.reshape(videos, patch_rows, model_width)
    step_onehot = (jnp.arange(TSTEPS, dtype=jnp.int32)[None, :] == steps_idx[:, None]).astype(
        jnp.float32
    )
    modulation_all = jnp.dot(step_onehot, modulation[0], precision=lax.Precision.HIGHEST)
    head_rows = jnp.dot(step_onehot, head_mod, precision=lax.Precision.HIGHEST)
    gain_rows = qk_gain[0]
    slot_iota = jnp.arange(patch_rows, dtype=jnp.int32)
    ring_counts = jnp.stack(
        [jnp.take(counts, (own_patch - k) % patch_count, axis=1) for k in range(patch_count)], axis=1
    )
    own_live = slot_iota[None, :] < ring_counts[:, :1]

    def counts_of(video):
        return lax.dynamic_index_in_dim(ring_counts, video, 0, keepdims=False)

    def project(hidden, video):
        mod = lax.dynamic_index_in_dim(modulation_all, video, 0)
        shift_vec = mod[:, :model_width]
        scale_vec = mod[:, model_width : 2 * model_width]
        normed = (layer_norm(hidden) * (1.0 + scale_vec) + shift_vec).astype(jnp.bfloat16)
        projected = jnp.dot(normed, proj_full, preferred_element_type=jnp.float32)
        queries = rms_norm(projected[:, :model_width], gain_rows[:model_width]).astype(jnp.bfloat16)
        keys = rms_norm(projected[:, model_width : 2 * model_width], gain_rows[model_width:])
        fresh_kv = jnp.concatenate(
            [keys.astype(jnp.bfloat16), projected[:, 2 * model_width :].astype(jnp.bfloat16)], axis=-1
        )
        return queries, fresh_kv

    def finish(hidden, attended, video):
        gate_vec = lax.dynamic_index_in_dim(modulation_all, video, 0)[:, 2 * model_width :]
        return hidden + gate_vec * jnp.dot(attended, out_full, preferred_element_type=jnp.float32)

    def attend_early(queries, fresh_kv):
        blocks = [(kv, 0, HEADS) for kv in [fresh_kv] + early_blocks]
        return attend(HEADS, queries, 0, blocks, counts_of(early))

    def head(hidden, video):
        head_in = (
            layer_norm(hidden) * (1.0 + head_rows[video, None, model_width:])
            + head_rows[video, None, :model_width]
        ).astype(jnp.bfloat16)
        velocity = jnp.dot(head_in, head_weight, preferred_element_type=jnp.float32)
        velocity = jnp.where(own_live[video][:, None], velocity, jnp.zeros_like(velocity))
        half_rows = patch_rows // 2
        returned = shifted(velocity[:half_rows].astype(jnp.bfloat16), "section", -1)
        return jnp.where(first_section, returned.astype(jnp.float32), velocity[half_rows:])

    def forward(hidden):
        return shifted(hidden.astype(jnp.bfloat16), "section", 1).astype(jnp.float32)

    def after(value, *earlier):
        return lax.optimization_barrier((value,) + earlier)[0]

    def send(value, pairs):
        return lax.ppermute(value, "patch", pairs)

    def pick(array, first_head, heads):
        first = first_head * HD
        return jnp.concatenate(
            [array[:, first : first + heads * HD], array[:, model_width + first : model_width + first + heads * HD]],
            axis=-1,
        )

    queries_a, fresh_a = project(start_hidden[0], early)
    late_stale = lax.dynamic_index_in_dim(stale_cache[0, :, 0], late, 0, keepdims=False)
    narrow = HEADS - WIDE
    halves = [pick(late_stale, first, WIDE // 2) for first in (0, WIDE // 2)]
    narrow_own = pick(late_stale, WIDE, narrow)
    queries_a, *halves = lax.optimization_barrier((queries_a, *halves))
    halves = [after(half, early_blocks[-1]) for half in halves]
    right_1 = [send(half, [(0, 1), (1, 2), (2, 3)]) for half in halves]
    left_1 = [send(half, [(3, 2), (2, 1), (1, 0)]) for half in halves]
    attended_a = attend_early(queries_a, fresh_a)
    attended_a, right_1[0], left_1[0] = lax.optimization_barrier((attended_a, right_1[0], left_1[0]))
    right_2 = [send(right_1[0], [(1, 2), (2, 3)]), None]
    left_2 = [send(left_1[0], [(2, 1), (1, 0)]), None]
    hidden_a = finish(start_hidden[0], attended_a, early)
    received = forward(hidden_a)
    hidden_b = jnp.where(first_section, start_hidden[1], received)
    hidden_b, right_1[1], left_1[1] = lax.optimization_barrier((hidden_b, right_1[1], left_1[1]))
    right_2[1] = send(right_1[1], [(1, 2), (2, 3)])
    left_2[1] = send(left_1[1], [(2, 1), (1, 0)])
    queries_b, fresh_b = project(hidden_b, late)
    queries_b, right_2[0], left_2[0] = lax.optimization_barrier((queries_b, right_2[0], left_2[0]))
    right_3 = [send(right_2[0], [(2, 3)]), None]
    left_3 = [send(left_2[0], [(1, 0)]), None]
    packed = jnp.concatenate([queries_b[:, WIDE * HD :], pick(fresh_b, WIDE, narrow)], axis=-1)
    guest = send(packed, [(0, 1), (3, 2)])
    right_3[1] = send(after(right_2[1], packed), [(2, 3)])
    left_3[1] = send(after(left_2[1], packed), [(1, 0)])
    narrow_own = after(narrow_own, right_2[0], left_2[0], queries_b)
    narrow_r1 = send(narrow_own, [(0, 1), (1, 2)])
    narrow_l1 = send(narrow_own, [(3, 2), (2, 1)])
    packed = jnp.concatenate([queries_b[:, WIDE * HD :], pick(fresh_b, WIDE, narrow)], axis=-1)
    guest = send(packed, [(0, 1), (3, 2)])
    narrow_r2 = send(narrow_r1, [(1, 2)])
    narrow_l2 = send(narrow_l1, [(2, 1)])
    narrow_2 = jnp.where(own_patch >= 2, narrow_r2, narrow_l2)
    guest_far = jnp.where(own_patch == 1, narrow_l1, narrow_r1)
    late_counts = counts_of(late)
    guest_patch = jnp.where(own_patch == 1, 1, 3)
    guest_counts = jnp.stack(
        [late_counts[guest_patch], late_counts[0], late_counts[2], late_counts[4 - guest_patch]]
    )
    guest_out = attend(
        narrow,
        guest,
        0,
        [
            (guest, narrow, 2 * narrow),
            (late_stale, WIDE, HEADS + WIDE),
            (narrow_2, 0, narrow),
            (guest_far, 0, narrow),
        ],
        guest_counts,
    )
    returned = send(guest_out, [(1, 0), (2, 3)])
    narrow_out = attend(
        narrow,
        queries_b,
        WIDE,
        [
            (fresh_b, WIDE, HEADS + WIDE),
            (narrow_r1, 0, narrow),
            (narrow_2, 0, narrow),
            (narrow_l1, 0, narrow),
        ],
        late_counts,
    )
    wide_out = [
        attend(
            WIDE // 2,
            queries_b,
            h * (WIDE // 2),
            [
                (fresh_b, h * (WIDE // 2), HEADS + h * (WIDE // 2)),
                (jnp.where(own_patch >= 1, right_1[h], left_3[h]), 0, WIDE // 2),
                (jnp.where(own_patch >= 2, right_2[h], left_2[h]), 0, WIDE // 2),
                (jnp.where(own_patch >= 3, right_3[h], left_1[h]), 0, WIDE // 2),
            ],
            late_counts,
        )
        for h in (0, 1)
    ]
    is_middle = (own_patch == 1) | (own_patch == 2)
    attended_b = jnp.concatenate([*wide_out, jnp.where(is_middle, narrow_out, returned)], axis=-1)
    hidden_b = finish(hidden_b, attended_b, late)
    received = forward(hidden_b)
    first_half = head(hidden_b, 0)
    queries_c, fresh_c = project(received, early)
    hidden_c = finish(received, attend_early(queries_c, fresh_c), early)
    second_half = head(hidden_c, 1)
    cache_buf = jnp.stack(
        [jnp.where(first_section, fresh_a, fresh_b), jnp.where(first_section, fresh_b, fresh_c)]
    )
    cache_buf = jnp.where(own_live[..., None], cache_buf, jnp.zeros_like(cache_buf))
    mine_half = jnp.stack([first_half, second_half])
    step_float = steps_idx.astype(jnp.float32)
    step_delta = sigma_of(step_float + 1.0) - sigma_of(step_float)
    new_latent = latent + step_delta[:, None, None, None] * mine_half[:, None]
    return (mine_half[:, None], new_latent, cache_buf[None, :, None])


def solution(mesh):
    in_specs = (
        P("fsdp", "patch", "section", None),
        P("fsdp", None),
        P("fsdp"),
        P(),
        P("section", "fsdp", None),
        P("section", "fsdp", None),
        P("section", None),
        P("section", None, None),
        P(),
        P(),
        P("section", "fsdp", "patch", None, None),
    )
    out_specs = (
        P("fsdp", "patch", "section", None),
        P("fsdp", "patch", "section", None),
        P("section", "fsdp", "patch", None, None),
    )
    return jax.shard_map(body, mesh=mesh, in_specs=in_specs, out_specs=out_specs, check_vma=False)
```

```python
import math

import jax
import jax.numpy as jnp
from jax import lax
from jax.experimental import pallas as pl
from jax.experimental.pallas import tpu as pltpu
from jax.sharding import PartitionSpec as P

HEADS = 12
HD = 128
TSTEPS = 50


EPS = 1e-06


def shifted(shard, axis, by):
    devices = lax.axis_size(axis)
    pairs = [(i, i + by) for i in range(devices) if 0 <= i + by < devices]
    return lax.ppermute(shard, axis, pairs)


def layer_norm(hidden):
    center = hidden - jnp.mean(hidden, axis=-1, keepdims=True)
    return center * lax.rsqrt(jnp.mean(center * center, axis=-1, keepdims=True) + EPS)


def rms_norm(values_in, gain_vec):
    return (
        values_in
        * lax.rsqrt(jnp.mean(values_in * values_in, axis=-1, keepdims=True) + EPS)
        * gain_vec
    )


def sigma_of(step_float):
    remain = 1.0 - step_float / TSTEPS
    return 5.0 * remain / (1.0 + 4.0 * remain)


HEADS_STEP = 2


def attend_kernel(counts_ref, q_ref, *refs):
    blocks = (len(refs) - 1) // 2
    out_ref = refs[-1]
    slot = lax.broadcasted_iota(jnp.int32, (1, refs[0].shape[0]), 1)
    bias = [jnp.where(slot < counts_ref[b], 0.0, -jnp.inf) for b in range(blocks)]
    for head in range(q_ref.shape[1] // HD):
        cols = slice(head * HD, (head + 1) * HD)
        query = q_ref[:, cols]
        scores = []
        for b in range(blocks):
            score = lax.dot_general(
                query, refs[2 * b][:, cols], (((1,), (1,)), ((), ())), preferred_element_type=jnp.float32
            )
            scores.append(score * (math.log2(math.e) / math.sqrt(HD)) + bias[b])
        top = scores[0]
        for score in scores[1:]:
            top = jnp.maximum(top, score)
        top = jnp.max(top, axis=1, keepdims=True)
        total = None
        mixed = None
        for b in range(blocks):
            weight = jnp.exp2(scores[b] - top)
            part = jnp.dot(
                weight.astype(jnp.bfloat16), refs[2 * b + 1][:, cols], preferred_element_type=jnp.float32
            )
            total = weight if total is None else total + weight
            mixed = part if mixed is None else mixed + part
        denom = jnp.sum(total, axis=1, keepdims=True)
        out_ref[:, cols] = (mixed / denom).astype(jnp.bfloat16)


def attend(heads, queries, q_head, kv_blocks, block_counts):
    rows = queries.shape[0]
    cols = HEADS_STEP * HD
    steps = heads // HEADS_STEP

    def spec(array, first_head):
        first = first_head // HEADS_STEP
        return pl.BlockSpec((array.shape[0], cols), lambda h: (0, h + first))

    specs = [pl.BlockSpec(memory_space=pltpu.SMEM), spec(queries, q_head)]
    operands = [block_counts, queries]
    for keys, key_head, values, value_head in kv_blocks:
        specs += [spec(keys, key_head), spec(values, value_head)]
        operands += [keys, values]
    keys = rows * len(kv_blocks)
    width = heads * HD
    return pl.pallas_call(
        attend_kernel,
        grid=(steps,),
        in_specs=specs,
        out_specs=pl.BlockSpec((rows, cols), lambda h: (0, h)),
        out_shape=jax.ShapeDtypeStruct((rows, width), jnp.bfloat16),
        cost_estimate=pl.CostEstimate(
            flops=4 * rows * keys * width,
            bytes_accessed=4 * (rows + keys) * width,
            transcendentals=rows * keys * heads,
        ),
    )(*operands)


def body(
    latent,
    counts,
    steps_idx,
    embed_weight,
    wqkv,
    wo,
    qk_gain,
    modulation,
    head_mod,
    head_weight,
    stale_cache,
):
    section_index = lax.axis_index("section")
    own_patch = lax.axis_index("patch")
    first_section = section_index == 0
    videos = latent.shape[0]
    assert videos == 2 and lax.axis_size("section") == 2 and counts.shape[1] == 4
    patch_rows = stale_cache.shape[3]
    model_width = embed_weight.shape[1]
    patch_count = counts.shape[1]
    early = section_index
    late = 1 - section_index
    rows_full = lax.all_gather(latent.astype(jnp.bfloat16), "section", axis=2, tiled=True)
    proj_full = lax.all_gather(wqkv[0], "fsdp", axis=0, tiled=True)
    out_full = lax.all_gather(wo[0], "fsdp", axis=0, tiled=True)
    ring = [(i, (i + 1) % patch_count) for i in range(patch_count)]

    def after(value, *earlier):
        return lax.optimization_barrier((value,) + earlier)[0]

    def step(block):
        return lax.ppermute(block, "patch", ring)

    def across(block, to_first):
        return lax.ppermute(block, "section", [(1, 0)] if to_first else [(0, 1)])

    early_stale = lax.dynamic_index_in_dim(stale_cache[0, :, 0], early, 0, keepdims=False)
    late_stale = lax.dynamic_index_in_dim(stale_cache[0, :, 0], late, 0, keepdims=False)
    early_keys, early_values = early_stale[:, :model_width], early_stale[:, model_width:]
    first_mix = jnp.where(first_section, early_keys, across(early_values, False))
    last_mix = jnp.where(first_section, across(early_values, True), early_keys)
    late_1 = step(late_stale)
    first_keys, first_values = [], []
    block = after(first_mix, late_1)
    for _ in range(patch_count - 1):
        block = step(block)
        first_keys.append(block)
        first_values.append(across(block, True))

    start_hidden = jnp.dot(
        rows_full.reshape(-1, rows_full.shape[3]), embed_weight, preferred_element_type=jnp.float32
    )
    start_hidden = start_hidden.reshape(videos, patch_rows, model_width)
    step_onehot = (jnp.arange(TSTEPS, dtype=jnp.int32)[None, :] == steps_idx[:, None]).astype(
        jnp.float32
    )
    modulation_all = jnp.dot(step_onehot, modulation[0], precision=lax.Precision.HIGHEST)
    head_rows = jnp.dot(step_onehot, head_mod, precision=lax.Precision.HIGHEST)
    gain_rows = qk_gain[0]
    slot_iota = jnp.arange(patch_rows, dtype=jnp.int32)
    ring_counts = jnp.stack(
        [jnp.take(counts, (own_patch - k) % patch_count, axis=1) for k in range(patch_count)], axis=1
    )
    own_live = slot_iota[None, :] < ring_counts[:, :1]

    def counts_of(video):
        return lax.dynamic_index_in_dim(ring_counts, video, 0, keepdims=False)

    def project(hidden, video):
        mod = lax.dynamic_index_in_dim(modulation_all, video, 0)
        shift_vec = mod[:, :model_width]
        scale_vec = mod[:, model_width : 2 * model_width]
        normed = (layer_norm(hidden) * (1.0 + scale_vec) + shift_vec).astype(jnp.bfloat16)
        projected = jnp.dot(normed, proj_full, preferred_element_type=jnp.float32)
        queries = rms_norm(projected[:, :model_width], gain_rows[:model_width]).astype(jnp.bfloat16)
        keys = rms_norm(projected[:, model_width : 2 * model_width], gain_rows[model_width:])
        fresh_kv = jnp.concatenate(
            [keys.astype(jnp.bfloat16), projected[:, 2 * model_width :].astype(jnp.bfloat16)], axis=-1
        )
        return queries, fresh_kv

    def finish(hidden, attended, video):
        gate_vec = lax.dynamic_index_in_dim(modulation_all, video, 0)[:, 2 * model_width :]
        return hidden + gate_vec * jnp.dot(attended, out_full, preferred_element_type=jnp.float32)

    def attend_with(queries, fresh_kv, keys, values, video):
        blocks = [(fresh_kv, 0, fresh_kv, HEADS)]
        for key, value in zip(keys, values):
            blocks.append((key, 0, value, value.shape[1] // HD - HEADS))
        return attend(HEADS, queries, 0, blocks, counts_of(video))

    def head(hidden, video):
        head_in = (
            layer_norm(hidden) * (1.0 + head_rows[video, None, model_width:])
            + head_rows[video, None, :model_width]
        ).astype(jnp.bfloat16)
        velocity = jnp.dot(head_in, head_weight, preferred_element_type=jnp.float32)
        velocity = jnp.where(own_live[video][:, None], velocity, jnp.zeros_like(velocity))
        half_rows = patch_rows // 2
        returned = shifted(velocity[:half_rows].astype(jnp.bfloat16), "section", -1)
        return jnp.where(first_section, returned.astype(jnp.float32), velocity[half_rows:])

    def forward(hidden):
        return shifted(hidden.astype(jnp.bfloat16), "section", 1).astype(jnp.float32)

    queries_a, fresh_a = project(start_hidden[0], early)
    late_2 = step(after(late_1, first_keys[-1]))
    attended_a = attend_with(queries_a, fresh_a, first_keys, first_values, early)
    late_3 = step(late_2)
    hidden_a = finish(start_hidden[0], attended_a, early)
    received = forward(hidden_a)
    hidden_b = jnp.where(first_section, start_hidden[1], received)
    queries_b, fresh_b = project(hidden_b, late)
    last_keys, last_values = [], []
    block = after(last_mix, late_3)
    for _ in range(patch_count - 1):
        block = step(block)
        last_keys.append(block)
        last_values.append(across(block, False))
    late_blocks = [late_1, late_2, late_3]
    attended_b = attend_with(queries_b, fresh_b, late_blocks, late_blocks, late)
    hidden_b = finish(hidden_b, attended_b, late)
    received = forward(hidden_b)
    first_half = head(hidden_b, 0)
    queries_c, fresh_c = project(received, early)
    attended_c = attend_with(queries_c, fresh_c, last_keys, last_values, early)
    hidden_c = finish(received, attended_c, early)
    second_half = head(hidden_c, 1)
    cache_buf = jnp.stack(
        [jnp.where(first_section, fresh_a, fresh_b), jnp.where(first_section, fresh_b, fresh_c)]
    )
    cache_buf = jnp.where(own_live[..., None], cache_buf, jnp.zeros_like(cache_buf))
    mine_half = jnp.stack([first_half, second_half])
    step_float = steps_idx.astype(jnp.float32)
    step_delta = sigma_of(step_float + 1.0) - sigma_of(step_float)
    new_latent = latent + step_delta[:, None, None, None] * mine_half[:, None]
    return (mine_half[:, None], new_latent, cache_buf[None, :, None])


def solution(mesh):
    in_specs = (
        P("fsdp", "patch", "section", None),
        P("fsdp", None),
        P("fsdp"),
        P(),
        P("section", "fsdp", None),
        P("section", "fsdp", None),
        P("section", None),
        P("section", None, None),
        P(),
        P(),
        P("section", "fsdp", "patch", None, None),
    )
    out_specs = (
        P("fsdp", "patch", "section", None),
        P("fsdp", "patch", "section", None),
        P("section", "fsdp", "patch", None, None),
    )
    return jax.shard_map(body, mesh=mesh, in_specs=in_specs, out_specs=out_specs, check_vma=False)
```
